32 devices in a mesh: band: 4 (over z), roster: 8 (over y, x, core).
Axes of the slice: x: 2, y: 2, z: 4, core: 2. Of those that a mesh axis runs over, the one named last changes fastest.
Arguments:
- tiles: bfloat16 [4, 8, 6, 256, 256], P('band', 'roster'), as said below
- tile_slots: int32 [4, 8, 6], P('band', 'roster'), may hold values from 0 to 5, each once within a row
- tile_count: int32 [4, 8], P('band', 'roster'), may hold values from 1 to 6, as said below
- costs: float32 [6144, 128], P('roster'), may hold values from 1000 to 10000
- primal_start: float32 [6144, 128], P('roster'), may hold values from 0 to 1
- dual_start: float32 [2048, 128], P('band'), may hold values from 0.5 to 4
Outputs:
- primal: float32 [6144, 128], P('roster')
- dual: float32 [2048, 128], P('band')
The draws below stay inside these ranges and needn't reach their ends.
Inputs may be any that keep to these rules, and one draw needn't show every extreme that they name: `tile_slots`: each device's slots list every tile position once; slot s is in use where s < tile_count. `tile_count`: some device uses all 6 slots. `tiles`: entries are zero or positive.
All inputs are finite; a program needn't handle non-finite values.
Results may differ from the reference program's by a relative error of at most 0.0003.
Values sent between devices are 32-bit elements; how exact they have to be, the bound alone decides.
A program may use at most 64 MiB of HBM per device.

```python
import math
import jax
import jax.numpy as jnp
from jax import lax

TILE = 256
SCEN = 128
ROUNDS = 3
ITERS = 4
TILES_DEV = 6
ROWS_DEV = 512
COLS_DEV = 768
DUTIES = 2048
ROSTERS = 6144
N_BAND = 4
N_ROSTER = 8


def draw_tiles(key, part):
    key_mask, key_value, key_row, key_col = jax.random.split(jax.random.fold_in(key, 11), 4)
    shape = (N_BAND, N_ROSTER, TILES_DEV, TILE, TILE)
    present = jax.random.bernoulli(key_mask, 0.35, shape).astype(jnp.float32)
    value = jnp.exp(jax.random.uniform(key_value, shape, jnp.float32, -0.7, 0.7))
    row_fac = jnp.exp(jax.random.uniform(key_row, (N_BAND, N_ROSTER, TILES_DEV, TILE, 1), jnp.float32, 0.0, math.log(10.0)))
    col_fac = jnp.exp(jax.random.uniform(key_col, (N_BAND, N_ROSTER, TILES_DEV, 1, TILE), jnp.float32, 0.0, math.log(10.0)))
    return (present * value * row_fac * col_fac).astype(jnp.bfloat16)


def draw_tile_count(key, part):
    key_count, key_full, key_other = jax.random.split(jax.random.fold_in(key, 23), 3)
    lowest = max(1, TILES_DEV // 4)
    total = N_BAND * N_ROSTER
    counts = jax.random.randint(key_count, (total,), lowest, TILES_DEV + 1, jnp.int32)
    full_at = jax.random.randint(key_full, (), 0, total, jnp.int32)
    low_at = (full_at + 1 + jax.random.randint(key_other, (), 0, total - 1, jnp.int32)) % total
    counts = counts.at[full_at].set(TILES_DEV).at[low_at].set(lowest)
    return counts.reshape(N_BAND, N_ROSTER)


def levels(stream_key, shape, cuts, least, high):
    level = 1.0
    for axis_at, blocks in cuts:
        steps = jax.random.uniform(jax.random.fold_in(jax.random.fold_in(stream_key, 6), axis_at), (blocks,), jnp.float32, least / len(cuts), high / len(cuts))
        level = level * jnp.repeat(jnp.exp(steps), shape[axis_at] // blocks).reshape((-1,) + (1,) * (len(shape) - 1 - axis_at))
    return level


def setup_inputs(seed: int = 0) -> dict:
    splits = jax.random.split(jax.random.key(seed), 7)
    tiles = draw_tiles(jax.random.fold_in(splits[6], 71), 0)
    tile_slots = jax.vmap(lambda own: jax.random.permutation(own, TILES_DEV))(jax.random.split(splits[1], N_BAND * N_ROSTER)).reshape((N_BAND, N_ROSTER, TILES_DEV)).astype(jnp.int32)
    tile_count = draw_tile_count(jax.random.fold_in(splits[6], 71), 0)
    costs = jnp.clip(jnp.exp(math.log(10000.0) - 2.3025851 * jax.random.uniform(splits[3], (ROSTERS, SCEN), jnp.float32) ** levels(splits[3], (ROSTERS, SCEN), ((0, 8),), -0.2, 0.2)), 1000.0, 10000.0)
    primal_start = jnp.clip(1.0 * jax.random.uniform(splits[4], (ROSTERS, SCEN), jnp.float32) ** levels(splits[4], (ROSTERS, SCEN), ((0, 8),), -0.2, 0.2), 0.0, 1.0)
    dual_start = jnp.clip(0.5 + 3.5 * jax.random.uniform(splits[5], (DUTIES, SCEN), jnp.float32) ** levels(splits[5], (DUTIES, SCEN), ((0, 4),), -0.2, 0.2), 0.5, 4.0)
    return dict(tiles=tiles, tile_slots=tile_slots, tile_count=tile_count, costs=costs, primal_start=primal_start, dual_start=dual_start)


HIGH = lax.Precision.HIGHEST
eps = 1e-06

def block_parts(tile_block, slot_list, count, row_scale, col_scale):
    tile = tile_block.shape[1]
    row_tiles = row_scale.shape[0] // tile
    col_tiles = col_scale.shape[0] // tile
    slots = slot_list.astype(jnp.int32)
    row_index = slots // col_tiles
    col_index = slots % col_tiles
    active = (jnp.arange(slots.shape[0], dtype=jnp.int32) < count).astype(jnp.float32)
    row_part = row_scale.reshape(row_tiles, tile)[row_index]
    col_part = col_scale.reshape(col_tiles, tile)[col_index]
    scaled = tile_block.astype(jnp.float32) * row_part[:, :, None] * col_part[:, None, :] * active[:, None, None]
    row_hot = (row_index[None, :] == jnp.arange(row_tiles, dtype=jnp.int32)[:, None]).astype(jnp.float32)
    col_hot = (col_index[None, :] == jnp.arange(col_tiles, dtype=jnp.int32)[:, None]).astype(jnp.float32)
    return (scaled, row_index, col_index, row_hot, col_hot)

def block_peaks(tile_block, slot_list, count, row_scale, col_scale):
    scaled, row_index, col_index, row_hot, col_hot = block_parts(tile_block, slot_list, count, row_scale, col_scale)
    magnitude = jnp.abs(scaled)
    slot_rows = lax.optimization_barrier(jnp.max(magnitude, axis=2))
    slot_cols = lax.optimization_barrier(jnp.max(magnitude, axis=1))
    row_peak = lax.optimization_barrier(jnp.max(row_hot[:, :, None] * slot_rows[None], axis=1)).reshape(-1)
    col_peak = lax.optimization_barrier(jnp.max(col_hot[:, :, None] * slot_cols[None], axis=1)).reshape(-1)
    return (row_peak, col_peak, jnp.sum(scaled * scaled))

def block_forward(tile_block, slot_list, count, row_scale, col_scale, extrapolated):
    scaled, row_index, col_index, row_hot, col_hot = block_parts(tile_block, slot_list, count, row_scale, col_scale)
    tile = scaled.shape[1]
    gathered = extrapolated.reshape(col_hot.shape[0], tile, -1)[col_index]
    product = jnp.einsum('sij,sjk->sik', scaled, gathered, precision=HIGH)
    return jnp.einsum('rs,sik->rik', row_hot, product, precision=HIGH).reshape(row_scale.shape[0], -1)

def block_backward(tile_block, slot_list, count, row_scale, col_scale, dual_rows):
    scaled, row_index, col_index, row_hot, col_hot = block_parts(tile_block, slot_list, count, row_scale, col_scale)
    tile = scaled.shape[1]
    gathered = dual_rows.reshape(row_hot.shape[0], tile, -1)[row_index]
    product = jnp.einsum('sij,sik->sjk', scaled, gathered, precision=HIGH)
    return jnp.einsum('cs,sjk->cjk', col_hot, product, precision=HIGH).reshape(col_scale.shape[0], -1)

def reference(tiles, tile_slots, tile_count, costs, primal_start, dual_start):
    row_scale = jnp.ones((N_BAND, ROWS_DEV), jnp.float32)
    col_scale = jnp.ones((N_ROSTER, COLS_DEV), jnp.float32)

    def all_peaks(row_scale, col_scale):

        def per_band(items):
            tile_b, slot_b, count_b, rscale_b = items
            return jax.vmap(lambda tb, sl, ct, cs: block_peaks(tb, sl, ct, rscale_b, cs))(tile_b, slot_b, count_b, col_scale)
        return lax.map(per_band, (tiles, tile_slots, tile_count, row_scale))
    for turn in range(ROUNDS):
        row_part, col_part, squares = all_peaks(row_scale, col_scale)
        row_peak = lax.optimization_barrier(jnp.max(row_part, axis=1))
        col_peak = lax.optimization_barrier(jnp.max(col_part, axis=0))
        row_scale = row_scale / jnp.sqrt(row_peak + eps)
        col_scale = col_scale / jnp.sqrt(col_peak + eps)
    row_part, col_part, squares = all_peaks(row_scale, col_scale)
    eta = 0.9 / jnp.sqrt(jnp.sum(squares) + eps)
    col_full = col_scale.reshape(-1)[:, None]
    row_full = row_scale.reshape(-1)[:, None]
    cost_t = costs * col_full
    upper = 1.0 / col_full
    primal = primal_start / col_full
    dual = dual_start / row_full
    for step in range(ITERS):
        dual_bands = dual.reshape(N_BAND, ROWS_DEV, -1)

        def back_step(total, items):
            tile_b, slot_b, count_b, rscale_b, dual_b = items
            terms = jax.vmap(lambda tb, sl, ct, cs: block_backward(tb, sl, ct, rscale_b, cs, dual_b))(tile_b, slot_b, count_b, col_scale)
            return (total + terms, None)
        init = jnp.zeros((N_ROSTER, COLS_DEV, dual.shape[1]), jnp.float32)
        g_whole, unused = lax.scan(back_step, init, (tiles, tile_slots, tile_count, row_scale, dual_bands))
        g_whole = g_whole.reshape(-1, dual.shape[1])
        primal_next = jnp.clip(primal - eta * (cost_t - g_whole), 0.0, upper)
        extrapolated = (2.0 * primal_next - primal).reshape(N_ROSTER, COLS_DEV, -1)

        def per_band(items):
            tile_b, slot_b, count_b, rscale_b = items
            terms = jax.vmap(lambda tb, sl, ct, cs, xb: block_forward(tb, sl, ct, rscale_b, cs, xb))(tile_b, slot_b, count_b, col_scale, extrapolated)
            return lax.optimization_barrier(jnp.sum(terms, axis=0))
        h_whole = lax.map(per_band, (tiles, tile_slots, tile_count, row_scale)).reshape(-1, dual.shape[1])
        dual = dual + eta * (row_full - h_whole)
        primal = primal_next
    return (primal, dual)
```

```python
import functools

import jax
import jax.numpy as jnp
from jax import lax
from jax.experimental import pallas as pl
from jax.experimental.pallas import tpu as pltpu
from jax.sharding import PartitionSpec as P

ROUNDS = 3
ITERS = 4
eps = 1e-06
GROUPS = 4
SHIFT = 2.0
SCATTER = 4.6
GATHER = 4.6
CAST = 4.0
DOWN = 2.0**-24
UP = 2.0**24
MESH = pl.DeviceIdType.MESH
f32 = jnp.float32
bf16 = jnp.bfloat16


def kernel(
    cfg, slots_ref, count_ref, tiles_ref, cost_ref, x0_ref, y0_ref, primal_ref, dual_ref,
    a_ref, at_ref, tile_s, tile_r, stage, cost_t, x_t, y_t, part, blocks, casts, fin, yfin,
    rpeak_s, rpeak_r, cpeak_s, cpeak_r, fr_s, fr_r, fb_s, fb_r, col_s, col_r, cols_v,
    rp_ss, rp_rs, cp_ss, cp_rs, fr_ss, fr_rs, fb_ss, fb_rs,
    rs_ss, rs_rs, ag_ss, ag_rs, h_ss, h_rs, pair_ss, pair_rs, xf_ss, xf_rs, yf_ss, yf_rs,
):
    nb, nr, groups = cfg
    z = lax.axis_index("band")
    r = lax.axis_index("roster")
    core = r % 2
    chip = r // 2
    chips = nr // 2
    slots = tiles_ref.shape[2]
    tile = tiles_ref.shape[3]
    rows, scen = y0_ref.shape
    cols = cost_ref.shape[0]
    col_tiles = cols // tile
    half = scen // 2
    per = half // groups
    both = 2 * cols
    width = both // nb

    def roster_peer(d):
        return (z, (r + d) % nr)

    def band_peer(d):
        return ((z + d) % nb, r)

    def chip_peer(d):
        return (z, 2 * ((chip + d) % chips) + core)

    partner = (z, r + 1 - 2 * core)

    barrier = pltpu.get_barrier_semaphore()
    for d in range(1, nr):
        pl.semaphore_signal(barrier, inc=1, device_id=roster_peer(d), device_id_type=MESH)
    for d in range(1, nb):
        pl.semaphore_signal(barrier, inc=1, device_id=band_peer(d), device_id_type=MESH)

    def build():
        for p in range(slots):
            at = jnp.int32(0)
            for s in range(slots):
                at = jnp.where(slots_ref[0, 0, s] == p, jnp.int32(s), at)
            factor = jnp.where(at < count_ref[0, 0], jnp.float32(DOWN), jnp.float32(0.0))
            block = tiles_ref[0, 0, at].astype(f32) * factor
            i, j = (p // col_tiles) * tile, (p % col_tiles) * tile
            tile_s[i : i + tile, j : j + tile] = block
            a_ref[i : i + tile, j : j + tile] = block.astype(bf16)
            at_ref[j : j + tile, i : i + tile] = block.T.astype(bf16)

    def fold(ref, at, span, factor, op):
        part = ref[at : at + 128, :span].astype(f32) * factor
        if op is jnp.add:
            part = part * part
        total = part[:, :128]
        for j in range(128, part.shape[1], 128):
            total = op(total, part[:, j : j + 128])
        return total.T

    def peaks(turn, row, col_up):
        for i in range(0, rows, 128):
            peak = jnp.max(fold(a_ref, i, cols, col_up, jnp.maximum), axis=0, keepdims=True)
            rpeak_s[turn, :, i : i + 128] = peak * row[:, i : i + 128]
        for j in range(0, cols, 128):
            peak = jnp.max(fold(at_ref, j, rows, row, jnp.maximum), axis=0, keepdims=True)
            cpeak_s[turn, :, j : j + 128] = peak * col_up[:, j : j + 128]

    def rpeak_copy(turn, d):
        return pltpu.make_async_remote_copy(
            rpeak_s.at[turn], rpeak_r.at[turn, d], rp_ss.at[turn, d], rp_rs.at[turn, d],
            device_id=roster_peer(d), device_id_type=MESH)

    def cpeak_copy(turn, d):
        return pltpu.make_async_remote_copy(
            cpeak_s.at[turn], cpeak_r.at[turn, d], cp_ss.at[turn, d], cp_rs.at[turn, d],
            device_id=band_peer(d), device_id_type=MESH)

    def peaks_send(turn):
        for d in range(1, nb):
            cpeak_copy(turn, d).start()
        for d in range(1, nr):
            rpeak_copy(turn, d).start()

    def peaks_wait(turn):
        row = rpeak_s[turn]
        col = cpeak_s[turn]
        for d in range(1, nr):
            rpeak_copy(turn, d).wait_recv()
            row = jnp.maximum(row, rpeak_r[turn, d])
        for d in range(1, nb):
            cpeak_copy(turn, d).wait_recv()
            col = jnp.maximum(col, cpeak_r[turn, d])
        return row, col

    def fr_copy(d):
        return pltpu.make_async_remote_copy(
            fr_s, fr_r.at[d], fr_ss.at[d], fr_rs.at[d],
            device_id=roster_peer(d), device_id_type=MESH)

    def fb_copy(d):
        return pltpu.make_async_remote_copy(
            fb_s, fb_r.at[d], fb_ss.at[d], fb_rs.at[d],
            device_id=band_peer(d), device_id_type=MESH)

    mine = pl.ds(pl.multiple_of(core * half, 8), half)
    theirs = pl.ds(pl.multiple_of((1 - core) * half, 8), half)

    def pair_copy(i, src, dst):
        return pltpu.make_async_remote_copy(
            src, dst, pair_ss.at[i], pair_rs.at[i], device_id=partner, device_id_type=MESH)

    def tile_copy():
        return pair_copy(0, tile_s, tile_r)

    def start_copy(i):
        dst = cost_t if i == 0 else x_t.at[0]
        return pair_copy(1 + i, stage.at[i, theirs], dst.at[:, cols:])

    def scale_copy():
        return pair_copy(3, col_s, col_r)

    def block_of(k):
        return pl.ds(pl.multiple_of(k * width, 128), width)

    def of(grp):
        return pl.ds(grp * per, per)

    def rs_copy(grp, d):
        return pltpu.make_async_remote_copy(
            part.at[of(grp), block_of((z + d) % nb)], blocks.at[d, of(grp)],
            rs_ss.at[grp, d], rs_rs.at[grp, d],
            device_id=band_peer(d), device_id_type=MESH)

    def ag_copy(grp, t, d):
        here = x_t.at[(t + 1) % 2, of(grp), block_of(z)]
        return pltpu.make_async_remote_copy(
            here, here, ag_ss.at[grp, d], ag_rs.at[grp, d],
            device_id=band_peer(d), device_id_type=MESH)

    def ag_arrived(grp, t, d):
        here = x_t.at[(t + 1) % 2, of(grp), block_of((z + nb - d) % nb)]
        return pltpu.make_async_remote_copy(
            here, here, ag_ss.at[grp, d], ag_rs.at[grp, d],
            device_id=band_peer(d), device_id_type=MESH)

    def h_copy(grp, t, d):
        here = casts.at[t % 2, chip, of(grp)]
        return pltpu.make_async_remote_copy(
            here, here, h_ss.at[grp, d], h_rs.at[t % 2, grp, d],
            device_id=chip_peer(d), device_id_type=MESH)

    def h_arrived(grp, t, d):
        here = casts.at[t % 2, (chip + chips - d) % chips, of(grp)]
        return pltpu.make_async_remote_copy(
            here, here, h_ss.at[grp, d], h_rs.at[t % 2, grp, d],
            device_id=chip_peer(d), device_id_type=MESH)

    def final_at(grp):
        return pl.ds(pl.multiple_of(core * half + grp * per, 8), per)

    def xf_copy(grp):
        return pltpu.make_async_remote_copy(
            x_t.at[ITERS % 2, of(grp), cols:], fin.at[final_at(grp)],
            xf_ss.at[grp], xf_rs.at[grp], device_id=partner, device_id_type=MESH)

    def yf_copy(grp):
        return pltpu.make_async_remote_copy(
            y_t.at[of(grp)], yfin.at[final_at(grp)],
            yf_ss.at[grp], yf_rs.at[grp], device_id=partner, device_id_type=MESH)

    def split_dot(value, matrix):
        high = value.astype(bf16)
        low = (value - high.astype(f32)).astype(bf16)
        both = jnp.dot(jnp.concatenate([high, low], 0), matrix, preferred_element_type=f32)
        return both[: value.shape[0]] + both[value.shape[0] :]

    far = range(nb - 1, 0, -1)
    state = {}

    def begin():
        state["row"] = jnp.ones((1, rows), f32)
        state["col_up"] = jnp.ones((1, cols), f32) * UP
        build()
        peaks(0, state["row"], state["col_up"])
        pl.semaphore_wait(barrier, nr - 1 + nb - 1)
        peaks_send(0)
        tile_copy().start()

    def starts():
        for i, ref in enumerate((cost_ref, x0_ref)):
            for j in range(0, cols, 128):
                stage[i, :, j : j + 128] = ref[j : j + 128, :].T
            start_copy(i).start()
        cost_t[:, :cols] = stage[0, mine]
        x_t[0, :, :cols] = stage[1, mine]
        for i in range(0, rows, 128):
            yfin[:, i : i + 128] = y0_ref[i : i + 128, :].T
        y_t[...] = yfin[mine]

    def tiles_in():
        tile_copy().wait_recv()
        for i in range(0, rows, tile):
            for j in range(0, cols, tile):
                block = tile_r[i : i + tile, j : j + tile]
                a_ref[i : i + tile, cols + j : cols + j + tile] = block.astype(bf16)
                at_ref[cols + j : cols + j + tile, i : i + tile] = block.T.astype(bf16)

    def starts_in():
        for i in range(2):
            start_copy(i).wait_recv()

    def equilibrate(turn):
        row_peak, col_peak = peaks_wait(turn)
        state["row"] = state["row"] / jnp.sqrt(row_peak + eps)
        state["col_up"] = state["col_up"] / jnp.sqrt(col_peak + eps)
        if turn + 1 < ROUNDS:
            peaks(turn + 1, state["row"], state["col_up"])
            peaks_send(turn + 1)
        else:
            squares_start()

    def squares_start():
        row, col_up = state["row"], state["col_up"]
        col_s[...] = col_up
        scale_copy().start()
        state["row_up"] = row * UP
        squares = jnp.zeros((1, 128), f32)
        for j in range(0, cols, 128):
            part = jnp.sum(fold(at_ref, j, rows, row, jnp.add), axis=0, keepdims=True)
            scale = col_up[:, j : j + 128]
            squares = squares + part * scale * scale
        fr_s[...] = squares
        for d in range(1, nr):
            fr_copy(d).start()
        state["squares"] = squares

    def squares_mid():
        squares = state["squares"]
        for d in range(1, nr):
            fr_copy(d).wait_recv()
            squares = squares + fr_r[d]
        fb_s[...] = squares
        for d in range(1, nb):
            fb_copy(d).start()
        state["squares"] = squares

    def scales_in():
        scale_copy().wait_recv()
        cols_v[:, :cols] = state["col_up"]
        cols_v[:, cols:] = col_r[...]
        state["up"] = cols_v[:, block_of(z)]
        col = state["up"] * DOWN
        cost_t[:, block_of(z)] = cost_t[:, block_of(z)] * col

    def squares_end():
        squares = state["squares"]
        for d in range(1, nb):
            fb_copy(d).wait_recv()
            squares = squares + fb_r[d]
        eta = 0.9 / jnp.sqrt(jnp.sum(squares, axis=1, keepdims=True) + eps)
        state["eta_col"] = eta * (state["up"] * DOWN)
        state["eta_row"] = eta * state["row"]

    def scatter(grp, t):
        if t > 0:
            for d in far:
                rs_copy(grp, d).wait_send()
        part[of(grp), :] = split_dot(y_t[of(grp), :], a_ref[...])
        for d in far:
            rs_copy(grp, d).start()

    def update(grp, t):
        total = part[of(grp), block_of(z)]
        for d in range(1, nb):
            rs_copy(grp, d).wait_recv()
            total = total + blocks[d, of(grp)]
        if t > 0:
            for d in far:
                ag_copy(grp, t - 1, d).wait_send()
        before = x_t[t % 2, of(grp), block_of(z)]
        cost = cost_t[of(grp), block_of(z)]
        move = state["eta_col"] * (cost - state["up"] * total)
        x_t[(t + 1) % 2, of(grp), block_of(z)] = jnp.clip(before - move, 0.0, 1.0)
        for d in far:
            ag_copy(grp, t, d).start()

    def cast(grp, t):
        for d in range(1, nb):
            ag_arrived(grp, t, d).wait_recv()
        after = x_t[(t + 1) % 2, of(grp), :]
        value = 2.0 * after - x_t[t % 2, of(grp), :]
        if t > 0:
            for d in range(1, chips):
                h_copy(grp, t - 1, d).wait_send()
        casts[t % 2, chip, of(grp)] = split_dot(value, at_ref[...])
        for d in range(1, chips):
            h_copy(grp, t, d).start()
        if t + 1 == ITERS:
            xf_copy(grp).start()

    def rise(grp, t):
        for d in range(1, chips):
            h_arrived(grp, t, d).wait_recv()
        total = casts[t % 2, 0, of(grp)]
        for k in range(1, chips):
            total = total + casts[t % 2, k, of(grp)]
        row, row_up, eta_row = state["row"], state["row_up"], state["eta_row"]
        y_t[of(grp), :] = y_t[of(grp), :] + eta_row * (row - row_up * total)
        if t + 1 < ITERS:
            scatter(grp, t + 1)
        else:
            yf_copy(grp).start()

    begin()
    starts()
    equilibrate(0)
    tiles_in()
    for grp in range(groups // 2):
        scatter(grp, 0)
    equilibrate(1)
    for grp in range(groups // 2, groups):
        scatter(grp, 0)
    starts_in()
    equilibrate(2)
    squares_mid()
    scales_in()
    squares_end()

    plan = []

    def put(when, step, *args):
        plan.append((when, len(plan), functools.partial(step, *args)))

    for grp in range(groups):
        when = grp * SHIFT
        for t in range(ITERS):
            put(when, update, grp, t)
            when += GATHER
            put(when, cast, grp, t)
            when += CAST
            put(when, rise, grp, t)
            when += SCATTER
    for when, index, step in sorted(plan, key=lambda entry: entry[:2]):
        step()

    col = state["col_up"] * DOWN
    row = state["row"]
    fin[mine, :] = x_t[ITERS % 2, :, :cols]
    for grp in range(groups):
        xf_copy(grp).wait_recv()
    for j in range(0, cols, 128):
        primal_ref[j : j + 128, :] = (fin[:, j : j + 128] / col[:, j : j + 128]).T
    yfin[mine, :] = y_t[...]
    for grp in range(groups):
        yf_copy(grp).wait_recv()
    for i in range(0, rows, 128):
        dual_ref[i : i + 128, :] = (yfin[:, i : i + 128] / row[:, i : i + 128]).T

    tile_copy().wait_send()
    scale_copy().wait_send()
    for i in range(2):
        start_copy(i).wait_send()
    for grp in range(groups):
        xf_copy(grp).wait_send()
        yf_copy(grp).wait_send()
        for d in far:
            rs_copy(grp, d).wait_send()
            ag_copy(grp, ITERS - 1, d).wait_send()
        for d in range(1, chips):
            h_copy(grp, ITERS - 1, d).wait_send()
    for d in range(1, nr):
        fr_copy(d).wait_send()
        for turn in range(ROUNDS):
            rpeak_copy(turn, d).wait_send()
    for d in range(1, nb):
        fb_copy(d).wait_send()
        for turn in range(ROUNDS):
            cpeak_copy(turn, d).wait_send()


def shards(nb, nr, tiles, tile_slots, tile_count, costs, primal_start, dual_start):
    rows, scen = dual_start.shape
    cols = costs.shape[0]
    groups = GROUPS
    half = scen // 2
    both = 2 * cols
    chips = nr // 2
    vmem = pl.BlockSpec(memory_space=pltpu.VMEM)
    smem = pl.BlockSpec(memory_space=pltpu.SMEM)
    dma = pltpu.SemaphoreType.DMA
    return pl.pallas_call(
        functools.partial(kernel, (nb, nr, groups)),
        name="primal_dual",
        out_shape=(
            jax.ShapeDtypeStruct((cols, scen), f32),
            jax.ShapeDtypeStruct((rows, scen), f32),
        ),
        in_specs=[smem, smem, vmem, vmem, vmem, vmem],
        out_specs=(vmem, vmem),
        scratch_shapes=[
            pltpu.VMEM((rows, both), bf16),
            pltpu.VMEM((both, rows), bf16),
            pltpu.VMEM((rows, cols), f32),
            pltpu.VMEM((rows, cols), f32),
            pltpu.VMEM((2, scen, cols), f32),
            pltpu.VMEM((half, both), f32),
            pltpu.VMEM((2, half, both), f32),
            pltpu.VMEM((half, rows), f32),
            pltpu.VMEM((half, both), f32),
            pltpu.VMEM((nb, half, both // nb), f32),
            pltpu.VMEM((2, chips, half, rows), f32),
            pltpu.VMEM((scen, cols), f32),
            pltpu.VMEM((scen, rows), f32),
            pltpu.VMEM((ROUNDS, 1, rows), f32),
            pltpu.VMEM((ROUNDS, nr, 1, rows), f32),
            pltpu.VMEM((ROUNDS, 1, cols), f32),
            pltpu.VMEM((ROUNDS, nb, 1, cols), f32),
            pltpu.VMEM((1, 128), f32),
            pltpu.VMEM((nr, 1, 128), f32),
            pltpu.VMEM((1, 128), f32),
            pltpu.VMEM((nb, 1, 128), f32),
            pltpu.VMEM((1, cols), f32),
            pltpu.VMEM((1, cols), f32),
            pltpu.VMEM((1, both), f32),
            dma((ROUNDS, nr)),
            dma((ROUNDS, nr)),
            dma((ROUNDS, nb)),
            dma((ROUNDS, nb)),
            dma((nr,)),
            dma((nr,)),
            dma((nb,)),
            dma((nb,)),
            dma((groups, nb)),
            dma((groups, nb)),
            dma((groups, nb)),
            dma((groups, nb)),
            dma((groups, chips)),
            dma((2, groups, chips)),
            dma((4,)),
            dma((4,)),
            dma((groups,)),
            dma((groups,)),
            dma((groups,)),
            dma((groups,)),
        ],
        compiler_params=pltpu.CompilerParams(collective_id=0, has_side_effects=True),
    )(tile_slots, tile_count, tiles, costs, primal_start, dual_start)


def solution(mesh):
    placed = (
        P("band", "roster", None, None, None),
        P("band", "roster", None),
        P("band", "roster"),
        P("roster", None),
        P("roster", None),
        P("band", None),
    )
    return jax.shard_map(
        functools.partial(shards, mesh.shape["band"], mesh.shape["roster"]),
        mesh=mesh,
        in_specs=placed,
        out_specs=(P("roster", None), P("band", None)),
        check_vma=False,
    )
```

```python
import functools

import jax
import jax.numpy as jnp
from jax import lax
from jax.experimental import pallas as pl
from jax.experimental.pallas import tpu as pltpu
from jax.sharding import PartitionSpec as P

ROUNDS = 3
ITERS = 4
eps = 1e-06
GROUPS = 4
SHIFT = 2.2
CROSS = 4.4
CAST = 4.2
FLAT = 64
DOWN = 2.0**-24
UP = 2.0**24
MESH = pl.DeviceIdType.MESH
f32 = jnp.float32
bf16 = jnp.bfloat16


def kernel(
    cfg, slots_ref, count_ref, tiles_ref, cost_ref, x0_ref, y0_ref, primal_ref, dual_ref,
    a_ref, at_ref, tile_s, tile_r, stage, ystage, cost_t, x_t, y_t, part, others, casts, fin, yfin,
    rpeak_s, rpeak_r, cpeak_s, cpeak_r, fr_s, fr_r, fb_s, fb_r, col_s, col_r, row_s, row_r,
    rp_ss, rp_rs, cp_ss, cp_rs, fr_ss, fr_rs, fb_ss, fb_rs,
    g_ss, g_rs, h_ss, h_rs, pair_ss, pair_rs, bulk_ss, bulk_rs, fwd_ss, fwd_rs,
    xf_ss, xf_rs, yf_ss, yf_rs,
):
    nb, nr, groups = cfg
    z = lax.axis_index("band")
    r = lax.axis_index("roster")
    core = r % 2
    chip = r // 2
    chips = nr // 2
    side = z % 2
    slots = tiles_ref.shape[2]
    tile = tiles_ref.shape[3]
    rows, scen = y0_ref.shape
    cols = cost_ref.shape[0]
    col_tiles = cols // tile
    quarter = scen // 4
    per = quarter // groups
    chunks = rows // 128
    flat = nb * nr <= FLAT

    def roster_peer(d):
        return (z, (r + d) % nr)

    def band_peer(d):
        return ((z + d) % nb, r)

    def any_peer(d):
        return ((z + d // nr) % nb, (r + d % nr) % nr)

    def chip_peer(d):
        return (z, 2 * ((chip + d) % chips) + core)

    def pair_peer(d):
        return ((z + 2 * d) % nb, r)

    partner = (z, r + 1 - 2 * core)
    below = (z + 1 - 2 * side, r)
    across = (z + 1 - 2 * side, r + 1 - 2 * core)

    barrier = pltpu.get_barrier_semaphore()
    if flat:
        greet = [any_peer(d) for d in range(1, nb * nr)]
    else:
        greet = [roster_peer(d) for d in range(1, nr)] + [band_peer(d) for d in range(1, nb)] + [across]
    for peer in greet:
        pl.semaphore_signal(barrier, inc=1, device_id=peer, device_id_type=MESH)

    def build():
        for p in range(slots):
            at = jnp.int32(0)
            for s in range(slots):
                at = jnp.where(slots_ref[0, 0, s] == p, jnp.int32(s), at)
            factor = jnp.where(at < count_ref[0, 0], jnp.float32(DOWN), jnp.float32(0.0))
            block = tiles_ref[0, 0, at].astype(f32) * factor
            i, j = (p // col_tiles) * tile, (p % col_tiles) * tile
            tile_s[i : i + tile, j : j + tile] = block
            a_ref[i : i + tile, j : j + tile] = block.astype(bf16)
            at_ref[j : j + tile, i : i + tile] = block.T.astype(bf16)

    def fold(ref, at, span, factor, op):
        part = ref[at : at + 128, :span].astype(f32) * factor
        if op is jnp.add:
            part = part * part
        total = part[:, :128]
        for j in range(128, part.shape[1], 128):
            total = op(total, part[:, j : j + 128])
        return total.T

    def peaks(turn, row, col_up):
        for i in range(0, rows, 128):
            peak = jnp.max(fold(a_ref, i, cols, col_up, jnp.maximum), axis=0, keepdims=True)
            rpeak_s[turn, :, i : i + 128] = peak * row[:, i : i + 128]
        for j in range(0, cols, 128):
            peak = jnp.max(fold(at_ref, j, rows, row, jnp.maximum), axis=0, keepdims=True)
            cpeak_s[turn, :, j : j + 128] = peak * col_up[:, j : j + 128]

    def rpeak_copy(turn, d):
        return pltpu.make_async_remote_copy(
            rpeak_s.at[turn], rpeak_r.at[turn, d], rp_ss.at[turn, d], rp_rs.at[turn, d],
            device_id=roster_peer(d), device_id_type=MESH)

    def cpeak_copy(turn, d):
        return pltpu.make_async_remote_copy(
            cpeak_s.at[turn], cpeak_r.at[turn, d], cp_ss.at[turn, d], cp_rs.at[turn, d],
            device_id=band_peer(d), device_id_type=MESH)

    def peaks_send(turn):
        for d in range(1, nb):
            cpeak_copy(turn, d).start()
        for d in range(1, nr):
            rpeak_copy(turn, d).start()

    def peaks_wait(turn):
        row = rpeak_s[turn]
        col = cpeak_s[turn]
        for d in range(1, nr):
            rpeak_copy(turn, d).wait_recv()
            row = jnp.maximum(row, rpeak_r[turn, d])
        for d in range(1, nb):
            cpeak_copy(turn, d).wait_recv()
            col = jnp.maximum(col, cpeak_r[turn, d])
        return row, col

    firsts = range(1, nb * nr if flat else nr)

    def fr_copy(d):
        return pltpu.make_async_remote_copy(
            fr_s, fr_r.at[d], fr_ss.at[d], fr_rs.at[d],
            device_id=any_peer(d) if flat else roster_peer(d), device_id_type=MESH)

    def fb_copy(d):
        return pltpu.make_async_remote_copy(
            fb_s, fb_r.at[d], fb_ss.at[d], fb_rs.at[d],
            device_id=band_peer(d), device_id_type=MESH)

    def set_at(side, core):
        return pl.ds(pl.multiple_of((2 * side + core) * quarter, 8), quarter)

    def send(i, peer, src, dst):
        return pltpu.make_async_remote_copy(
            src, dst, pair_ss.at[i], pair_rs.at[i], device_id=peer, device_id_type=MESH)

    def tile_copy():
        return send(0, partner, tile_s, tile_r.at[0])

    def cost_copy():
        return send(1, partner, stage.at[0, set_at(side, 1 - core)], cost_t.at[:, cols:])

    def x0_copy():
        return send(2, partner, stage.at[1, set_at(side, 1 - core)], x_t.at[:, cols:])

    def y0_copy():
        return send(3, below, ystage.at[set_at(1 - side, core)], y_t.at[:, rows:])

    def col_copy():
        return send(4, partner, col_s, col_r)

    def row_copy():
        return send(5, below, row_s, row_r)

    def bulk_copy(k):
        at = pl.ds(k * 128, 128)
        return pltpu.make_async_remote_copy(
            tile_s.at[at], tile_r.at[1, at], bulk_ss.at[k], bulk_rs.at[k],
            device_id=below, device_id_type=MESH)

    def fwd_copy(k):
        at = pl.ds(k * 128, 128)
        return pltpu.make_async_remote_copy(
            tile_r.at[1, at], tile_r.at[2, at], fwd_ss.at[k], fwd_rs.at[k],
            device_id=partner, device_id_type=MESH)

    def of(grp):
        return pl.ds(grp * per, per)

    def g_copy(grp, t, d):
        return pltpu.make_async_remote_copy(
            part.at[of(grp)], others.at[t % 2, d, of(grp)],
            g_ss.at[grp, d], g_rs.at[t % 2, grp, d],
            device_id=pair_peer(d), device_id_type=MESH)

    def h_copy(grp, t, d):
        here = casts.at[t % 2, chip, of(grp)]
        return pltpu.make_async_remote_copy(
            here, here, h_ss.at[grp, d], h_rs.at[t % 2, grp, d],
            device_id=chip_peer(d), device_id_type=MESH)

    def h_arrived(grp, t, d):
        here = casts.at[t % 2, (chip + chips - d) % chips, of(grp)]
        return pltpu.make_async_remote_copy(
            here, here, h_ss.at[grp, d], h_rs.at[t % 2, grp, d],
            device_id=chip_peer(d), device_id_type=MESH)

    def final_at(grp):
        return pl.ds(pl.multiple_of((2 * side + core) * quarter + grp * per, 8), per)

    def x_copy(grp, i):
        src = x_t.at[of(grp), :cols] if i == 1 else x_t.at[of(grp), cols:]
        return pltpu.make_async_remote_copy(
            src, fin.at[final_at(grp)], xf_ss.at[grp, i], xf_rs.at[grp, i],
            device_id=(partner, below, across)[i], device_id_type=MESH)

    def y_copy(grp, i):
        src = y_t.at[of(grp), :rows] if i == 0 else y_t.at[of(grp), rows:]
        return pltpu.make_async_remote_copy(
            src, yfin.at[final_at(grp)], yf_ss.at[grp, i], yf_rs.at[grp, i],
            device_id=(partner, below, across)[i], device_id_type=MESH)

    def split_dot(value, matrix):
        high = value.astype(bf16)
        low = (value - high.astype(f32)).astype(bf16)
        both = jnp.dot(jnp.concatenate([high, low], 0), matrix, preferred_element_type=f32)
        return both[: value.shape[0]] + both[value.shape[0] :]

    state = {}

    def begin():
        state["row"] = jnp.ones((1, rows), f32)
        state["col_up"] = jnp.ones((1, cols), f32) * UP
        build()
        peaks(0, state["row"], state["col_up"])
        pl.semaphore_wait(barrier, len(greet))
        peaks_send(0)
        tile_copy().start()
        bulk_copy(0).start()

    def starts():
        for i in range(0, rows, 128):
            ystage[:, i : i + 128] = y0_ref[i : i + 128, :].T
        y0_copy().start()
        y_t[:, :rows] = ystage[set_at(side, core)]
        for i, ref in enumerate((cost_ref, x0_ref)):
            for j in range(0, cols, 128):
                stage[i, :, j : j + 128] = ref[j : j + 128, :].T
        cost_copy().start()
        x0_copy().start()
        cost_t[:, :cols] = stage[0, set_at(side, core)]
        x_t[:, :cols] = stage[1, set_at(side, core)]

    def place(block, i, j, high):
        a_ref[i : i + high, j : j + tile] = block.astype(bf16)
        at_ref[j : j + tile, i : i + high] = block.T.astype(bf16)

    def tiles_in():
        tile_copy().wait_recv()
        for i in range(0, rows, 128):
            for j in range(0, cols, tile):
                place(tile_r[0, i : i + 128, j : j + tile], i, cols + j, 128)

    def bulk_in(k):
        bulk_copy(k).wait_recv()
        fwd_copy(k).start()
        for j in range(0, cols, tile):
            place(tile_r[1, k * 128 : (k + 1) * 128, j : j + tile], rows + k * 128, j, 128)

    def fwd_in(k):
        fwd_copy(k).wait_recv()
        for j in range(0, cols, tile):
            place(tile_r[2, k * 128 : (k + 1) * 128, j : j + tile], rows + k * 128, cols + j, 128)

    def equilibrate(turn):
        row_peak, col_peak = peaks_wait(turn)
        state["row"] = state["row"] / jnp.sqrt(row_peak + eps)
        state["col_up"] = state["col_up"] / jnp.sqrt(col_peak + eps)
        if turn + 1 < ROUNDS:
            peaks(turn + 1, state["row"], state["col_up"])
            peaks_send(turn + 1)
        else:
            squares_start()

    def squares_start():
        row, col_up = state["row"], state["col_up"]
        squares = jnp.zeros((1, 128), f32)
        for j in range(0, cols, 128):
            part = jnp.sum(fold(at_ref, j, rows, row, jnp.add), axis=0, keepdims=True)
            scale = col_up[:, j : j + 128]
            squares = squares + part * scale * scale
        fr_s[...] = squares
        for d in reversed(firsts):
            fr_copy(d).start()
        state["squares"] = squares
        row_s[...] = row
        row_copy().start()
        col_s[...] = col_up
        col_copy().start()

    def squares_end():
        squares = state["squares"]
        for d in firsts:
            fr_copy(d).wait_recv()
            squares = squares + fr_r[d]
        if not flat:
            fb_s[...] = squares
            for d in range(1, nb):
                fb_copy(d).start()
            for d in range(1, nb):
                fb_copy(d).wait_recv()
                squares = squares + fb_r[d]
        eta = 0.9 / jnp.sqrt(jnp.sum(squares, axis=1, keepdims=True) + eps)
        col_copy().wait_recv()
        row_copy().wait_recv()
        up = jnp.concatenate([state["col_up"], col_r[...]], 1)
        wide = jnp.concatenate([state["row"], row_r[...]], 1)
        col = up * DOWN
        state["up"], state["wide"], state["wide_up"] = up, wide, wide * UP
        state["eta_col"], state["eta_row"] = eta * col, eta * wide
        cost_copy().wait_recv()
        x0_copy().wait_recv()
        cost_t[...] = cost_t[...] * col

    def scatter(grp, t):
        if t > 0:
            for d in range(1, nb // 2):
                g_copy(grp, t - 1, d).wait_send()
        part[of(grp), :] = split_dot(y_t[of(grp), :], a_ref[...])
        for d in range(1, nb // 2):
            g_copy(grp, t, d).start()

    def cast(grp, t):
        total = part[of(grp), :]
        for d in range(1, nb // 2):
            g_copy(grp, t, d).wait_recv()
            total = total + others[t % 2, d, of(grp)]
        before = x_t[of(grp), :]
        move = state["eta_col"] * (cost_t[of(grp), :] - state["up"] * total)
        after = jnp.clip(before - move, 0.0, 1.0)
        x_t[of(grp), :] = after
        if t > 0:
            for d in range(1, chips):
                h_copy(grp, t - 1, d).wait_send()
        casts[t % 2, chip, of(grp)] = split_dot(2.0 * after - before, at_ref[...])
        for d in range(1, chips):
            h_copy(grp, t, d).start()
        if t + 1 == ITERS:
            for i in range(3):
                x_copy(grp, i).start()

    def rise(grp, t):
        for d in range(1, chips):
            h_arrived(grp, t, d).wait_recv()
        total = casts[t % 2, 0, of(grp)]
        for k in range(1, chips):
            total = total + casts[t % 2, k, of(grp)]
        wide, wide_up, eta_row = state["wide"], state["wide_up"], state["eta_row"]
        y_t[of(grp), :] = y_t[of(grp), :] + eta_row * (wide - wide_up * total)
        if t + 1 < ITERS:
            scatter(grp, t + 1)
        else:
            for i in range(3):
                y_copy(grp, i).start()

    def bulk_start(k):
        bulk_copy(k).start()

    begin()
    starts()
    tiles_in()
    equilibrate(0)
    bulk_start(1)
    bulk_in(0)
    equilibrate(1)
    bulk_start(2)
    fwd_in(0)
    bulk_in(1)
    equilibrate(2)
    for k in range(3, chunks):
        bulk_copy(k).start()
    fwd_in(1)
    bulk_in(2)
    squares_end()
    fwd_in(2)
    for k in range(3, chunks):
        bulk_in(k)
    y0_copy().wait_recv()
    for k in range(3, chunks):
        fwd_in(k)

    plan = []

    def put(when, step, *args):
        plan.append((when, len(plan), functools.partial(step, *args)))

    for grp in range(groups):
        when = grp * SHIFT
        put(-1.0, scatter, grp, 0)
        for t in range(ITERS):
            put(when, cast, grp, t)
            when += CAST
            put(when, rise, grp, t)
            when += CROSS
    for when, index, step in sorted(plan, key=lambda entry: entry[:2]):
        step()

    col = state["col_up"] * DOWN
    row = state["row"]

    def finish_x():
        fin[set_at(side, core), :] = x_t[:, :cols]
        for grp in range(groups):
            for i in range(3):
                x_copy(grp, i).wait_recv()
        for j in range(0, cols, 128):
            primal_ref[j : j + 128, :] = (fin[:, j : j + 128] / col[:, j : j + 128]).T

    def finish_y():
        yfin[set_at(side, core), :] = y_t[:, :rows]
        for grp in range(groups):
            for i in range(3):
                y_copy(grp, i).wait_recv()
        for i in range(0, rows, 128):
            dual_ref[i : i + 128, :] = (yfin[:, i : i + 128] / row[:, i : i + 128]).T

    finish_x()
    finish_y()

    for copy in (tile_copy, cost_copy, x0_copy, y0_copy, col_copy, row_copy):
        copy().wait_send()
    for k in range(chunks):
        bulk_copy(k).wait_send()
        fwd_copy(k).wait_send()
    for grp in range(groups):
        for i in range(3):
            x_copy(grp, i).wait_send()
            y_copy(grp, i).wait_send()
        for d in range(1, nb // 2):
            g_copy(grp, ITERS - 1, d).wait_send()
        for d in range(1, chips):
            h_copy(grp, ITERS - 1, d).wait_send()
    for d in firsts:
        fr_copy(d).wait_send()
    for turn in range(ROUNDS):
        for d in range(1, nr):
            rpeak_copy(turn, d).wait_send()
        for d in range(1, nb):
            cpeak_copy(turn, d).wait_send()
    if not flat:
        for d in range(1, nb):
            fb_copy(d).wait_send()


def shards(nb, nr, tiles, tile_slots, tile_count, costs, primal_start, dual_start):
    rows, scen = dual_start.shape
    cols = costs.shape[0]
    groups = GROUPS
    quarter = scen // 4
    chips = nr // 2
    chunks = rows // 128
    firsts = nb * nr if nb * nr <= FLAT else nr
    vmem = pl.BlockSpec(memory_space=pltpu.VMEM)
    smem = pl.BlockSpec(memory_space=pltpu.SMEM)
    dma = pltpu.SemaphoreType.DMA
    return pl.pallas_call(
        functools.partial(kernel, (nb, nr, groups)),
        name="primal_dual",
        out_shape=(
            jax.ShapeDtypeStruct((cols, scen), f32),
            jax.ShapeDtypeStruct((rows, scen), f32),
        ),
        in_specs=[smem, smem, vmem, vmem, vmem, vmem],
        out_specs=(vmem, vmem),
        scratch_shapes=[
            pltpu.VMEM((2 * rows, 2 * cols), bf16),
            pltpu.VMEM((2 * cols, 2 * rows), bf16),
            pltpu.VMEM((rows, cols), f32),
            pltpu.VMEM((3, rows, cols), f32),
            pltpu.VMEM((2, scen, cols), f32),
            pltpu.VMEM((scen, rows), f32),
            pltpu.VMEM((quarter, 2 * cols), f32),
            pltpu.VMEM((quarter, 2 * cols), f32),
            pltpu.VMEM((quarter, 2 * rows), f32),
            pltpu.VMEM((quarter, 2 * cols), f32),
            pltpu.VMEM((2, nb // 2, quarter, 2 * cols), f32),
            pltpu.VMEM((2, chips, quarter, 2 * rows), f32),
            pltpu.VMEM((scen, cols), f32),
            pltpu.VMEM((scen, rows), f32),
            pltpu.VMEM((ROUNDS, 1, rows), f32),
            pltpu.VMEM((ROUNDS, nr, 1, rows), f32),
            pltpu.VMEM((ROUNDS, 1, cols), f32),
            pltpu.VMEM((ROUNDS, nb, 1, cols), f32),
            pltpu.VMEM((1, 128), f32),
            pltpu.VMEM((firsts, 1, 128), f32),
            pltpu.VMEM((1, 128), f32),
            pltpu.VMEM((nb, 1, 128), f32),
            pltpu.VMEM((1, cols), f32),
            pltpu.VMEM((1, cols), f32),
            pltpu.VMEM((1, rows), f32),
            pltpu.VMEM((1, rows), f32),
            dma((ROUNDS, nr)),
            dma((ROUNDS, nr)),
            dma((ROUNDS, nb)),
            dma((ROUNDS, nb)),
            dma((firsts,)),
            dma((firsts,)),
            dma((nb,)),
            dma((nb,)),
            dma((groups, nb // 2)),
            dma((2, groups, nb // 2)),
            dma((groups, chips)),
            dma((2, groups, chips)),
            dma((6,)),
            dma((6,)),
            dma((chunks,)),
            dma((chunks,)),
            dma((chunks,)),
            dma((chunks,)),
            dma((groups, 3)),
            dma((groups, 3)),
            dma((groups, 3)),
            dma((groups, 3)),
        ],
        compiler_params=pltpu.CompilerParams(collective_id=0, has_side_effects=True),
    )(tile_slots, tile_count, tiles, costs, primal_start, dual_start)


def solution(mesh):
    placed = (
        P("band", "roster", None, None, None),
        P("band", "roster", None),
        P("band", "roster"),
        P("roster", None),
        P("roster", None),
        P("band", None),
    )
    return jax.shard_map(
        functools.partial(shards, mesh.shape["band"], mesh.shape["roster"]),
        mesh=mesh,
        in_specs=placed,
        out_specs=(P("roster", None), P("band", None)),
        check_vma=False,
    )
```
